32 devices in a mesh: blk: 8 (over y, x, core), cross: 4 (over z).
Axes of the slice: x: 2, y: 2, z: 4, core: 2. Of those that a mesh axis runs over, the one named last changes fastest.
Arguments:
- receiver_spectra: float32 [4096, 2, 1024], P(('blk', 'cross')), may hold values from -400 to 400
- source_spectra: float32 [4096, 2, 1024], P(('blk', 'cross')), may hold values from -400 to 400
- quality: int32 [4096], P(('blk', 'cross')), may hold values 0 or 1
- slot_order: int32 [32, 128], P(('blk', 'cross')), may hold values from 0 to 127, each once within a row
- owners: int32 [2, 8], replicated, may hold values from 0 to 3
Outputs:
- correlations: bfloat16 [2, 8, 4, 128, 128, 256], P(None, 'blk', 'cross')
The draws below stay inside these ranges and needn't reach their ends.
Inputs may be any that keep to these rules, and one draw needn't show every extreme that they name: `slot_order`: each row is a permutation of 0 to 127.
All inputs are finite; a program needn't handle non-finite values. No bound on the sum of `quality` on one device may be relied on, other than what follows from the above.
Results may differ from the reference program's by a relative error of at most 0.0056.
Values sent between devices are 32-bit elements; how exact they have to be, the bound alone decides.
A program may use at most 128 MiB of HBM per device.

```python
import math
import jax
import jax.numpy as jnp
from jax import lax

F = 1024
L = 256
STEPS = 2
R = 128
P_SIZE = 128
RCV_ALL = 4096
SRC_ALL = 4096
N_BLK = 8
N_CROSS = 4


def spectra_law(key, rows):
    first, second, third = jax.random.split(key, 3)
    base = jnp.clip(jax.random.normal(first, (rows, 2, F), jnp.float32), -3.0, 3.0)
    row_scale = jnp.exp(jax.random.uniform(second, (rows, 1, 1), jnp.float32, 0.0, math.log(10.0)))
    bin_scale = jnp.exp(jax.random.uniform(third, (1, 1, F), jnp.float32, 0.0, math.log(10.0)))
    return base * row_scale * bin_scale


def draw_receiver_spectra(key, part):
    return spectra_law(jax.random.fold_in(key, 11), RCV_ALL)


def draw_source_spectra(key, part):
    return spectra_law(jax.random.fold_in(key, 23), SRC_ALL)


def touch_ends(values, key, low, top_value):
    shape = values.shape
    place = [jax.random.randint(jax.random.fold_in(key, axis), (), 0, shape[axis]) for axis in range(len(shape))]
    values = values.at[tuple(place)].set(low)
    longest = shape.index(max(shape))
    place[longest] = (place[longest] + 1) % shape[longest]
    return values.at[tuple(place)].set(top_value)


def setup_inputs(seed: int = 0) -> dict:
    arg_keys = jax.random.split(jax.random.key(seed), 6)
    receiver_spectra = draw_receiver_spectra(jax.random.fold_in(arg_keys[5], 71), 0)
    source_spectra = draw_source_spectra(jax.random.fold_in(arg_keys[5], 71), 0)
    quality = touch_ends((jax.random.randint(arg_keys[2], (RCV_ALL,), 0, 8) < 7).astype(jnp.int32), jax.random.fold_in(arg_keys[2], 1), 0, 1)
    slot_order = jax.vmap(lambda own: jax.random.permutation(own, R))(jax.random.split(arg_keys[3], (N_BLK * N_CROSS))).reshape((N_BLK * N_CROSS, R)).astype(jnp.int32)
    owners = touch_ends(jax.random.randint(arg_keys[4], (STEPS, N_BLK), 0, N_CROSS), jax.random.fold_in(arg_keys[4], 1), 0, N_CROSS - 1).astype(jnp.int32)
    return {"receiver_spectra": receiver_spectra, "source_spectra": source_spectra, "quality": quality, "slot_order": slot_order, "owners": owners}


def lag_tables(bins, lags):
    bin_index = jnp.arange(bins, dtype=jnp.int32)
    odd_index = 2 * jnp.arange(lags // 2, dtype=jnp.int32) + 1
    phase_turns = jnp.mod(bin_index[:, None] * odd_index[None, :], 4 * bins).astype(jnp.float32)
    phase_angle = phase_turns * (math.pi / (2 * bins))
    cos_table = (jnp.cos(phase_angle) / bins).astype(jnp.bfloat16)
    sin_table = (-jnp.sin(phase_angle) / bins).astype(jnp.bfloat16)
    return (cos_table, sin_table)

def whiten(spectra):
    mean_power = lax.optimization_barrier(jnp.mean(spectra * spectra, axis=(1, 2), keepdims=True))
    return spectra * lax.rsqrt(mean_power + 1e-06)

def correlate(panel_spec, slab_spec, cos_table, sin_table):
    npanel = panel_spec.shape[0]
    nslab = slab_spec.shape[0]
    width = math.gcd(npanel, 16)
    blocks = panel_spec.reshape(npanel // width, width, 2, panel_spec.shape[2])

    def one_block(source):
        inphase = source[:, None, 0, :] * slab_spec[None, :, 0, :] + source[:, None, 1, :] * slab_spec[None, :, 1, :]
        quadrature = source[:, None, 1, :] * slab_spec[None, :, 0, :] - source[:, None, 0, :] * slab_spec[None, :, 1, :]
        inphase = inphase.astype(jnp.bfloat16).reshape(width * nslab, -1)
        quadrature = quadrature.astype(jnp.bfloat16).reshape(width * nslab, -1)
        even = jnp.dot(inphase, cos_table, preferred_element_type=jnp.float32)
        odd = jnp.dot(quadrature, sin_table, preferred_element_type=jnp.float32)
        joined = jnp.concatenate([even + odd, even - odd], axis=-1).astype(jnp.bfloat16)
        return joined.reshape(width, nslab, -1)
    lagged = lax.map(one_block, blocks)
    return lagged.reshape(npanel, nslab, lagged.shape[-1])

def reference(receiver_spectra, source_spectra, quality, slot_order, owners):
    cos_table, sin_table = lag_tables(F, L)
    groups = N_BLK * N_CROSS
    kept = quality.astype(jnp.float32)[:, None, None]
    receivers = (whiten(receiver_spectra) * kept).reshape(groups, R, 2, F)
    receivers = jax.vmap(lambda slab_spec, order: slab_spec[order])(receivers, slot_order.reshape(groups, R))
    blocks = receivers.reshape(N_BLK, N_CROSS, R, 2, F)
    sources = whiten(source_spectra).reshape(N_BLK, N_CROSS, P_SIZE, 2, F)
    results = []
    for loop_step in range(STEPS):
        moved = jnp.roll(blocks, loop_step, axis=0).reshape(groups, R, 2, F)
        chosen = jax.vmap(lambda panels, owner: panels[owner])(sources, owners[loop_step])
        chosen = jnp.broadcast_to(chosen[:, None], (N_BLK, N_CROSS, P_SIZE, 2, F)).reshape(groups, P_SIZE, 2, F)
        lagged = lax.map(lambda pair: correlate(pair[0], pair[1], cos_table, sin_table), (chosen, moved))
        results.append(lagged.reshape(N_BLK, N_CROSS, P_SIZE, R, L))
    return jnp.stack(results)
```

```python
import functools
import math

import jax
import jax.numpy as jnp
import numpy as np
from jax import lax
from jax.experimental import pallas as pl
from jax.experimental.pallas import tpu as pltpu
from jax.sharding import PartitionSpec as P

L = 256
STEPS = 2
FINE = 16


def phase_tables(bins, coarse):
    bin_index = np.arange(bins, dtype=np.float64)[None, :]
    fine_angle = np.pi / bins * (np.arange(FINE)[:, None] + 0.5) * bin_index
    coarse_angle = np.pi / bins * (FINE * np.arange(coarse)[:, None]) * bin_index
    fine = np.stack([np.cos(fine_angle), np.sin(fine_angle)])
    slow = np.stack([np.cos(coarse_angle), np.sin(coarse_angle)]) / bins
    return jnp.asarray(fine, jnp.float32), jnp.asarray(slow, jnp.float32)


def whiten(spectra):
    mean_power = jnp.mean(spectra * spectra, axis=(1, 2), keepdims=True)
    return spectra * lax.rsqrt(mean_power + 1e-06)


def build_columns(slab, slow_ref, w_ref):
    bins = slow_ref.shape[2]
    slots = slab.shape[0]
    real, imag = slab[:, :bins], slab[:, bins:]
    for a in range(slow_ref.shape[1]):
        c, s = slow_ref[0, a : a + 1, :], slow_ref[1, a : a + 1, :]
        rc, rs, ic, is_ = real * c, real * s, imag * c, imag * s
        rows = slice(a * slots, (a + 1) * slots)
        w_ref[0, rows, :bins] = (rc + is_).astype(jnp.bfloat16)
        w_ref[0, rows, bins:] = (ic - rs).astype(jnp.bfloat16)
        w_ref[1, rows, :bins] = (rc - is_).astype(jnp.bfloat16)
        w_ref[1, rows, bins:] = (ic + rs).astype(jnp.bfloat16)


def build_rows(panel, fine_ref, x_ref):
    bins = fine_ref.shape[2]
    c, s = fine_ref[0], fine_ref[1]
    for p in range(panel.shape[0]):
        real, imag = panel[p : p + 1, :bins], panel[p : p + 1, bins:]
        rc, rs, ic, is_ = real * c, real * s, imag * c, imag * s
        rows = slice(p * FINE, (p + 1) * FINE)
        x_ref[0, rows, :bins] = (rc - is_).astype(jnp.bfloat16)
        x_ref[0, rows, bins:] = (rs + ic).astype(jnp.bfloat16)
        x_ref[1, rows, :bins] = (rc + is_).astype(jnp.bfloat16)
        x_ref[1, rows, bins:] = (ic - rs).astype(jnp.bfloat16)


def products(x_ref, w_ref, out_ref, channels, slots, coarse):
    half = coarse * FINE
    for sign in range(2):
        found = lax.dot_general(
            x_ref[sign], w_ref[sign], (((1,), (1,)), ((), ())), preferred_element_type=jnp.float32
        )
        for p in range(channels):
            part = found[p * FINE : (p + 1) * FINE]
            lags = jnp.concatenate([part[:, a * slots : (a + 1) * slots] for a in range(coarse)], axis=0)
            out_ref[p, :, sign * half : (sign + 1) * half] = lags.T.astype(jnp.bfloat16)


def kernel(coarse, s_ref, q_ref, fine_ref, slow_ref, out_ref, w_ref, x_ref):
    slots = q_ref.shape[1]
    channels = s_ref.shape[1]

    @pl.when(pl.program_id(1) == 0)
    def _():
        build_columns(q_ref[0], slow_ref, w_ref)

    build_rows(s_ref[0], fine_ref, x_ref)
    products(x_ref, w_ref, out_ref.at[0], channels, slots, coarse)


def correlate(panels, slabs, channels=16):
    steps, npanel, width = panels.shape
    nslab = slabs.shape[1]
    coarse = L // 2 // FINE
    fine, slow = phase_tables(width // 2, coarse)
    return pl.pallas_call(
        functools.partial(kernel, coarse),
        grid=(steps, npanel // channels),
        in_specs=[
            pl.BlockSpec((1, channels, width), lambda s, i: (s, i, 0)),
            pl.BlockSpec((1, nslab, width), lambda s, i: (s, 0, 0)),
            pl.BlockSpec(fine.shape, lambda s, i: (0, 0, 0)),
            pl.BlockSpec(slow.shape, lambda s, i: (0, 0, 0)),
        ],
        out_specs=pl.BlockSpec((1, channels, nslab, L), lambda s, i: (s, i, 0, 0)),
        out_shape=jax.ShapeDtypeStruct((steps, npanel, nslab, L), jnp.bfloat16),
        scratch_shapes=[
            pltpu.VMEM((2, coarse * nslab, width), jnp.bfloat16),
            pltpu.VMEM((2, channels * FINE, width), jnp.bfloat16),
        ],
        compiler_params=pltpu.CompilerParams(vmem_limit_bytes=56 << 20),
    )(panels, slabs, fine, slow)


def passed_along(value, axis, steps):
    count = lax.axis_size(axis)
    pairs = [(source, (source + steps) % count) for source in range(count)]
    return lax.ppermute(value, axis, pairs)


def local(receiver_spectra, source_spectra, quality, slot_order, owners):
    npanel, _, bins = source_spectra.shape
    kept = quality.astype(jnp.float32)[:, None, None]
    receivers = whiten(receiver_spectra) * kept
    receivers = jnp.take(receivers, slot_order[0], axis=0).reshape(-1, 2 * bins)
    sources = whiten(source_spectra).reshape(-1, 2 * bins)
    block_index = lax.axis_index("blk")
    my_owners = lax.dynamic_index_in_dim(owners, block_index, 1, keepdims=False)
    every_panel = lax.all_gather(sources, "cross", axis=0)
    panels = jnp.take(every_panel, my_owners, axis=0)
    slabs = jnp.stack([receivers, passed_along(receivers, "blk", 1)])
    return correlate(panels, slabs)[:, None, None]


def solution(mesh):
    placed = (
        P(("blk", "cross"), None, None),
        P(("blk", "cross"), None, None),
        P(("blk", "cross")),
        P(("blk", "cross"), None),
        P(),
    )
    return jax.shard_map(
        local,
        mesh=mesh,
        in_specs=placed,
        out_specs=P(None, "blk", "cross", None, None, None),
        check_vma=False,
    )
```

```python
import functools
import math

import jax
import jax.numpy as jnp
import numpy as np
from jax import lax
from jax.experimental import pallas as pl
from jax.experimental.pallas import tpu as pltpu
from jax.sharding import PartitionSpec as P

L = 256
STEPS = 2
FINE = 16
PIECE = 8
HOP = 2
MESH = pl.DeviceIdType.MESH


def phase_tables(bins, coarse):
    bin_index = np.arange(bins, dtype=np.float64)[None, :]
    fine_angle = np.pi / bins * (np.arange(FINE)[:, None] + 0.5) * bin_index
    coarse_angle = np.pi / bins * (FINE * np.arange(coarse)[:, None]) * bin_index
    fine = np.stack([np.cos(fine_angle), np.sin(fine_angle)])
    slow = np.stack([np.cos(coarse_angle), np.sin(coarse_angle)]) / bins
    return jnp.asarray(fine, jnp.float32), jnp.asarray(slow, jnp.float32)


def whiten(spectra):
    mean_power = jnp.mean(spectra * spectra, axis=(1, 2), keepdims=True)
    return spectra * lax.rsqrt(mean_power + 1e-06)


def build_columns(slab, slow_ref, w_ref):
    bins = slow_ref.shape[2]
    slots = slab.shape[0]
    real, imag = slab[:, :bins], slab[:, bins:]
    for a in range(slow_ref.shape[1]):
        c, s = slow_ref[0, a : a + 1, :], slow_ref[1, a : a + 1, :]
        rc, rs, ic, is_ = real * c, real * s, imag * c, imag * s
        rows = slice(a * slots, (a + 1) * slots)
        w_ref[0, rows, :bins] = (rc + is_).astype(jnp.bfloat16)
        w_ref[0, rows, bins:] = (ic - rs).astype(jnp.bfloat16)
        w_ref[1, rows, :bins] = (rc - is_).astype(jnp.bfloat16)
        w_ref[1, rows, bins:] = (ic + rs).astype(jnp.bfloat16)


def build_rows(panel, fine_ref, x_ref):
    bins = fine_ref.shape[2]
    c, s = fine_ref[0], fine_ref[1]
    for p in range(panel.shape[0]):
        real, imag = panel[p : p + 1, :bins], panel[p : p + 1, bins:]
        rc, rs, ic, is_ = real * c, real * s, imag * c, imag * s
        rows = slice(p * FINE, (p + 1) * FINE)
        x_ref[0, rows, :bins] = (rc - is_).astype(jnp.bfloat16)
        x_ref[0, rows, bins:] = (rs + ic).astype(jnp.bfloat16)
        x_ref[1, rows, :bins] = (rc + is_).astype(jnp.bfloat16)
        x_ref[1, rows, bins:] = (ic - rs).astype(jnp.bfloat16)


def product(x_ref, w_ref, out_ref, sign, channels, slots, coarse):
    half = coarse * FINE
    found = lax.dot_general(
        x_ref[sign], w_ref[sign], (((1,), (1,)), ((), ())), preferred_element_type=jnp.float32
    )
    for p in range(channels):
        part = found[p * FINE : (p + 1) * FINE]
        lags = jnp.concatenate([part[:, a * slots : (a + 1) * slots] for a in range(coarse)], axis=0)
        out_ref[p, :, sign * half : (sign + 1) * half] = lags.T.astype(jnp.bfloat16)


def kernel(
    coarse, channels, count, ring, owner_ref, own_ref, q_ref, fine_ref, slow_ref, out_ref,
    w_ref, x_ref, low, high, near, low_send, low_recv, high_send, high_recv, q_send, q_recv,
):
    step, block = pl.program_id(0), pl.program_id(1)
    npanel, slots = own_ref.shape[0], q_ref.shape[0]
    per_step = npanel // PIECE
    total = STEPS * per_step
    per_block = channels // PIECE
    blocks = npanel // channels
    me, spot = lax.axis_index("cross"), lax.axis_index("blk")
    has_low, has_high = me > 0, me < count - 1
    following, previous = lax.rem(spot + 1, ring), lax.rem(spot + ring - 1, ring)

    def own_rows(j):
        return pl.ds(pl.multiple_of(lax.rem(j, per_step) * PIECE, PIECE), PIECE)

    def upward(j, source):
        return pltpu.make_async_remote_copy(
            src_ref=source, dst_ref=low.at[j], send_sem=low_send.at[j], recv_sem=low_recv.at[j],
            device_id={"blk": spot, "cross": me + 1}, device_id_type=MESH,
        )

    def downward(j, source):
        return pltpu.make_async_remote_copy(
            src_ref=source, dst_ref=high.at[j], send_sem=high_send.at[j], recv_sem=high_recv.at[j],
            device_id={"blk": spot, "cross": me - 1}, device_id_type=MESH,
        )

    def slab_copy():
        return pltpu.make_async_remote_copy(
            src_ref=q_ref, dst_ref=near, send_sem=q_send.at[0], recv_sem=q_recv.at[0],
            device_id={"blk": following, "cross": me}, device_id_type=MESH,
        )

    def relay(t):
        up, down = t - HOP * (me - 1), t - HOP * (count - 2 - me)
        up_on = has_low & (up >= 0) & (up < total)
        down_on = has_high & (down >= 0) & (down < total)

        @pl.when(up_on)
        def _():
            upward(up, low.at[up]).wait_recv()
            mine = owner_ref[up // per_step] == me
            low[up] = jnp.where(mine, own_ref[own_rows(up), :], low[up])

        @pl.when(down_on)
        def _():
            downward(down, high.at[down]).wait_recv()
            mine = owner_ref[down // per_step] == me
            high[down] = jnp.where(mine, own_ref[own_rows(down), :], high[down])

        @pl.when(up_on & has_high)
        def _():
            upward(up, low.at[up]).start()

        @pl.when(down_on & has_low)
        def _():
            downward(down, high.at[down]).start()

    lead = HOP * (count - 2) + per_block

    @pl.when((step == 0) & (block == 0))
    def _():
        barrier = pltpu.get_barrier_semaphore()
        pl.semaphore_signal(barrier, inc=1, device_id={"blk": following, "cross": me}, device_id_type=MESH)
        pl.semaphore_signal(barrier, inc=1, device_id={"blk": previous, "cross": me}, device_id_type=MESH)

        @pl.when(has_low)
        def _():
            pl.semaphore_signal(barrier, inc=1, device_id={"blk": spot, "cross": me - 1}, device_id_type=MESH)

        @pl.when(has_high)
        def _():
            pl.semaphore_signal(barrier, inc=1, device_id={"blk": spot, "cross": me + 1}, device_id_type=MESH)

        pl.semaphore_wait(barrier, 2 + has_low.astype(jnp.int32) + has_high.astype(jnp.int32))

        @pl.when(me == 0)
        def _():
            @pl.loop(0, total)
            def _(j):
                upward(j, own_ref.at[own_rows(j), :]).start()

        @pl.when(me == count - 1)
        def _():
            @pl.loop(0, total)
            def _(j):
                downward(j, own_ref.at[own_rows(j), :]).start()

        slab_copy().start()

        @pl.when(me == 0)
        def _():
            @pl.loop(0, total)
            def _(j):
                low[j] = own_ref[own_rows(j), :]

        @pl.when(me == count - 1)
        def _():
            @pl.loop(0, total)
            def _(j):
                high[j] = own_ref[own_rows(j), :]

        build_columns(q_ref[...], slow_ref, w_ref)

        @pl.loop(0, lead)
        def _(t):
            relay(t)

    @pl.when((step == 1) & (block == 0))
    def _():
        slab_copy().wait()
        build_columns(near[...], slow_ref, w_ref)

    now = (step * blocks + block) * per_block
    above = owner_ref[step] > me
    panel = jnp.concatenate([jnp.where(above, high[now + j], low[now + j]) for j in range(per_block)], axis=0)
    mean_power = jnp.mean(panel * panel, axis=1, keepdims=True)
    build_rows(panel * lax.rsqrt(mean_power + 1e-06), fine_ref, x_ref)
    for sign in range(2):
        product(x_ref, w_ref, out_ref.at[0], sign, channels, slots, coarse)
        for extra in range(per_block // 2):
            relay(now + lead + sign * (per_block // 2) + extra)

    @pl.when((step == STEPS - 1) & (block == blocks - 1))
    def _():
        @pl.when(has_high)
        def _():
            @pl.loop(0, total)
            def _(j):
                upward(j, low.at[j]).wait_send()

        @pl.when(has_low)
        def _():
            @pl.loop(0, total)
            def _(j):
                downward(j, high.at[j]).wait_send()


def correlate(owners, sources, slab, count, ring, channels=16):
    npanel, width = sources.shape
    nslab = slab.shape[0]
    coarse = L // 2 // FINE
    fine, slow = phase_tables(width // 2, coarse)
    total = STEPS * npanel // PIECE
    whole = pl.BlockSpec(memory_space=pltpu.VMEM)
    pieces = pltpu.VMEM((total, PIECE, width), jnp.float32)
    many = pltpu.SemaphoreType.DMA((total,))
    one = pltpu.SemaphoreType.DMA((1,))
    return pl.pallas_call(
        functools.partial(kernel, coarse, channels, count, ring),
        grid=(STEPS, npanel // channels),
        in_specs=[pl.BlockSpec(memory_space=pltpu.SMEM), whole, whole, whole, whole],
        out_specs=pl.BlockSpec((1, channels, nslab, L), lambda s, i: (s, i, 0, 0)),
        out_shape=jax.ShapeDtypeStruct((STEPS, npanel, nslab, L), jnp.bfloat16),
        scratch_shapes=[
            pltpu.VMEM((2, coarse * nslab, width), jnp.bfloat16),
            pltpu.VMEM((2, channels * FINE, width), jnp.bfloat16),
            pieces, pieces, pltpu.VMEM((nslab, width), jnp.float32),
            many, many, many, many, one, one,
        ],
        compiler_params=pltpu.CompilerParams(
            vmem_limit_bytes=56 << 20, collective_id=0, has_side_effects=True
        ),
    )(owners, sources, slab, fine, slow)


def local(receiver_spectra, source_spectra, quality, slot_order, owners):
    bins = source_spectra.shape[2]
    kept = quality.astype(jnp.float32)[:, None, None]
    receivers = whiten(receiver_spectra) * kept
    receivers = jnp.take(receivers, slot_order[0], axis=0).reshape(-1, 2 * bins)
    sources = source_spectra.reshape(-1, 2 * bins)
    my_owners = lax.dynamic_index_in_dim(owners, lax.axis_index("blk"), 1, keepdims=False)
    count, ring = lax.axis_size("cross"), lax.axis_size("blk")
    return correlate(my_owners, sources, receivers, count, ring)[:, None, None]


def solution(mesh):
    placed = (
        P(("blk", "cross"), None, None),
        P(("blk", "cross"), None, None),
        P(("blk", "cross")),
        P(("blk", "cross"), None),
        P(),
    )
    return jax.shard_map(
        local,
        mesh=mesh,
        in_specs=placed,
        out_specs=P(None, "blk", "cross", None, None, None),
        check_vma=False,
    )
```

```python
import functools
import math

import jax
import jax.numpy as jnp
import numpy as np
from jax import lax
from jax.experimental import pallas as pl
from jax.experimental.pallas import tpu as pltpu
from jax.sharding import PartitionSpec as P

L = 256
STEPS = 2
FINE = 16
PIECE = 8
HOP = 2
GROUP = 4
MESH = pl.DeviceIdType.MESH


def phase_tables(bins, coarse):
    bin_index = np.arange(bins, dtype=np.float64)[None, :]
    fine_angle = np.pi / bins * (np.arange(FINE)[:, None] + 0.5) * bin_index
    coarse_angle = np.pi / bins * (FINE * np.arange(coarse)[:, None]) * bin_index
    fine = np.stack([np.cos(fine_angle), np.sin(fine_angle)])
    slow = np.stack([np.cos(coarse_angle), np.sin(coarse_angle)]) / bins
    return jnp.asarray(fine, jnp.float32), jnp.asarray(slow, jnp.float32)


def ordered(spectra, kept, slot_order):
    mean_power = jnp.mean(spectra * spectra, axis=1, keepdims=True)
    scaled = spectra * lax.rsqrt(mean_power + 1e-06) * kept
    coarse_part = scaled.astype(jnp.bfloat16)
    fine_part = (scaled - coarse_part.astype(jnp.float32)).astype(jnp.bfloat16)
    count = spectra.shape[0]
    picks = slot_order == lax.broadcasted_iota(jnp.int32, (count, count), 1)
    picks = jnp.where(picks, 1.0, 0.0).astype(jnp.bfloat16)
    first = jnp.dot(picks, coarse_part, preferred_element_type=jnp.float32)
    return first + jnp.dot(picks, fine_part, preferred_element_type=jnp.float32)


def build_columns(slab, slow_ref, w_ref):
    bins = slow_ref.shape[2]
    slots = slab.shape[0]
    real, imag = slab[:, :bins], slab[:, bins:]
    for a in range(slow_ref.shape[1]):
        c, s = slow_ref[0, a : a + 1, :], slow_ref[1, a : a + 1, :]
        rc, rs, ic, is_ = real * c, real * s, imag * c, imag * s
        rows = slice(a * slots, (a + 1) * slots)
        w_ref[0, rows, :bins] = (rc + is_).astype(jnp.bfloat16)
        w_ref[0, rows, bins:] = (ic - rs).astype(jnp.bfloat16)
        w_ref[1, rows, :bins] = (rc - is_).astype(jnp.bfloat16)
        w_ref[1, rows, bins:] = (ic + rs).astype(jnp.bfloat16)


def build_rows(panel, fine_ref, x_ref):
    bins = fine_ref.shape[2]
    c, s = fine_ref[0], fine_ref[1]
    for p in range(panel.shape[0]):
        real, imag = panel[p : p + 1, :bins], panel[p : p + 1, bins:]
        rc, rs, ic, is_ = real * c, real * s, imag * c, imag * s
        rows = slice(p * FINE, (p + 1) * FINE)
        x_ref[0, rows, :bins] = (rc - is_).astype(jnp.bfloat16)
        x_ref[0, rows, bins:] = (rs + ic).astype(jnp.bfloat16)
        x_ref[1, rows, :bins] = (rc + is_).astype(jnp.bfloat16)
        x_ref[1, rows, bins:] = (ic - rs).astype(jnp.bfloat16)


def product(x_ref, w_ref, out_ref, sign, channels, slots, coarse):
    half = coarse * FINE
    found = lax.dot_general(
        x_ref[sign], w_ref[sign], (((1,), (1,)), ((), ())), preferred_element_type=jnp.float32
    )
    for p in range(channels):
        part = found[p * FINE : (p + 1) * FINE]
        lags = jnp.concatenate([part[:, a * slots : (a + 1) * slots] for a in range(coarse)], axis=0)
        out_ref[p, :, sign * half : (sign + 1) * half] = lags.T.astype(jnp.bfloat16)


def kernel(
    coarse, channels, count, ring, owner_ref, own_ref, raw_ref, kept_ref, order_ref, fine_ref, slow_ref,
    out_ref, rows_ref, slabs_ref, w_ref, x_ref, q_ref, low, high, near, low_send, low_recv, high_send, high_recv, q_send, q_recv,
):
    step, block = pl.program_id(0), pl.program_id(1)
    npanel, slots = own_ref.shape[0], q_ref.shape[0]
    per_step = npanel // PIECE
    total = STEPS * per_step
    per_block = channels // PIECE
    blocks = npanel // channels
    me, spot = lax.axis_index("cross"), lax.axis_index("blk")
    has_low, has_high = me > 0, me < count - 1
    following, previous = lax.rem(spot + 1, ring), lax.rem(spot + ring - 1, ring)

    def own_rows(j):
        return pl.ds(pl.multiple_of(lax.rem(j, per_step) * PIECE, PIECE), PIECE)

    def upward(j, source):
        return pltpu.make_async_remote_copy(
            src_ref=source, dst_ref=low.at[j], send_sem=low_send.at[j], recv_sem=low_recv.at[j],
            device_id={"blk": spot, "cross": me + 1}, device_id_type=MESH,
        )

    def downward(j, source):
        return pltpu.make_async_remote_copy(
            src_ref=source, dst_ref=high.at[j], send_sem=high_send.at[j], recv_sem=high_recv.at[j],
            device_id={"blk": spot, "cross": me - 1}, device_id_type=MESH,
        )

    def slab_copy():
        return pltpu.make_async_remote_copy(
            src_ref=q_ref, dst_ref=near, send_sem=q_send.at[0], recv_sem=q_recv.at[0],
            device_id={"blk": following, "cross": me}, device_id_type=MESH,
        )

    def relay(t):
        up, down = t - HOP * (me - 1), t - HOP * (count - 2 - me)
        up_on = has_low & (up >= 0) & (up < total)
        down_on = has_high & (down >= 0) & (down < total)

        @pl.when(up_on)
        def _():
            upward(up, low.at[up]).wait_recv()
            mine = owner_ref[up // per_step] == me
            low[up] = jnp.where(mine, own_ref[own_rows(up), :], low[up])

        @pl.when(down_on)
        def _():
            downward(down, high.at[down]).wait_recv()
            mine = owner_ref[down // per_step] == me
            high[down] = jnp.where(mine, own_ref[own_rows(down), :], high[down])

        @pl.when(up_on & has_high)
        def _():
            upward(up, low.at[up]).start()

        @pl.when(down_on & has_low)
        def _():
            downward(down, high.at[down]).start()

    lead = HOP * (count - 2) + per_block

    @pl.when((step == 0) & (block == 0))
    def _():
        barrier = pltpu.get_barrier_semaphore()
        pl.semaphore_signal(barrier, inc=1, device_id={"blk": following, "cross": me}, device_id_type=MESH)
        pl.semaphore_signal(barrier, inc=1, device_id={"blk": previous, "cross": me}, device_id_type=MESH)

        @pl.when(has_low)
        def _():
            pl.semaphore_signal(barrier, inc=1, device_id={"blk": spot, "cross": me - 1}, device_id_type=MESH)

        @pl.when(has_high)
        def _():
            pl.semaphore_signal(barrier, inc=1, device_id={"blk": spot, "cross": me + 1}, device_id_type=MESH)

        pl.semaphore_wait(barrier, 2 + has_low.astype(jnp.int32) + has_high.astype(jnp.int32))

        @pl.when(me == 0)
        def _():
            @pl.loop(0, total)
            def _(j):
                upward(j, own_ref.at[own_rows(j), :]).start()

        @pl.when(me == count - 1)
        def _():
            @pl.loop(0, total)
            def _(j):
                downward(j, own_ref.at[own_rows(j), :]).start()

        @pl.when(me == 0)
        def _():
            @pl.loop(0, total)
            def _(j):
                low[j] = own_ref[own_rows(j), :]

        @pl.when(me == count - 1)
        def _():
            @pl.loop(0, total)
            def _(j):
                high[j] = own_ref[own_rows(j), :]

        q_ref[...] = ordered(raw_ref[...], kept_ref[...], order_ref[...])
        slabs_ref[0] = q_ref[...]
        build_columns(q_ref[...], slow_ref, w_ref)
        slab_copy().start()

        @pl.loop(0, lead)
        def _(t):
            relay(t)

    @pl.when((step == 1) & (block == 0))
    def _():
        slab_copy().wait()
        slabs_ref[1] = near[...]
        build_columns(near[...], slow_ref, w_ref)

    now = (step * blocks + block) * per_block
    above = owner_ref[step] > me
    panel = jnp.concatenate([jnp.where(above, high[now + j], low[now + j]) for j in range(per_block)], axis=0)
    mean_power = jnp.mean(panel * panel, axis=1, keepdims=True)
    panel = panel * lax.rsqrt(mean_power + 1e-06)
    later = lax.rem(block, GROUP) == GROUP - 1

    @pl.when(later)
    def _():
        rows_ref[0] = panel

    @pl.when(jnp.logical_not(later))
    def _():
        build_rows(panel, fine_ref, x_ref)

    for sign in range(2):
        @pl.when(jnp.logical_not(later))
        def _():
            product(x_ref, w_ref, out_ref.at[0], sign, channels, slots, coarse)

        for extra in range(per_block // 2):
            relay(now + lead + sign * (per_block // 2) + extra)

    @pl.when((step == STEPS - 1) & (block == blocks - 1))
    def _():
        @pl.when(has_high)
        def _():
            @pl.loop(0, total)
            def _(j):
                upward(j, low.at[j]).wait_send()

        @pl.when(has_low)
        def _():
            @pl.loop(0, total)
            def _(j):
                downward(j, high.at[j]).wait_send()


def finish(coarse, done_ref, rows_ref, slab_ref, fine_ref, slow_ref, out_ref, w_ref, x_ref):
    channels, slots = rows_ref.shape[1], slab_ref.shape[1]

    @pl.when(pl.program_id(1) == 0)
    def _():
        build_columns(slab_ref[0], slow_ref, w_ref)

    build_rows(rows_ref[0], fine_ref, x_ref)
    out_ref[: GROUP - 1] = done_ref[...]
    for sign in range(2):
        product(x_ref, w_ref, out_ref.at[GROUP - 1], sign, channels, slots, coarse)


def correlate(owners, sources, raw, kept, order, count, ring, channels=16):
    npanel, width = sources.shape
    nslab = raw.shape[0]
    coarse = L // 2 // FINE
    fine, slow = phase_tables(width // 2, coarse)
    total = STEPS * npanel // PIECE
    blocks = npanel // channels
    groups = blocks // GROUP
    whole = pl.BlockSpec(memory_space=pltpu.VMEM)
    pieces = pltpu.VMEM((total, PIECE, width), jnp.float32)
    slab = pltpu.VMEM((nslab, width), jnp.float32)
    many = pltpu.SemaphoreType.DMA((total,))
    one = pltpu.SemaphoreType.DMA((1,))
    columns = pltpu.VMEM((2, coarse * nslab, width), jnp.bfloat16)
    rotated = pltpu.VMEM((2, channels * FINE, width), jnp.bfloat16)
    kept_blocks = groups * (GROUP - 1)

    def kept_index(s, i):
        return (s * kept_blocks + i // GROUP * (GROUP - 1) + jnp.minimum(i % GROUP, GROUP - 2), 0, 0, 0)

    done, rows, slabs = pl.pallas_call(
        functools.partial(kernel, coarse, channels, count, ring),
        grid=(STEPS, blocks),
        in_specs=[pl.BlockSpec(memory_space=pltpu.SMEM)] + [whole] * 6,
        out_specs=[
            pl.BlockSpec((1, channels, nslab, L), kept_index),
            pl.BlockSpec((1, channels, width), lambda s, i: (s * groups + i // GROUP, 0, 0)),
            whole,
        ],
        out_shape=[
            jax.ShapeDtypeStruct((STEPS * kept_blocks, channels, nslab, L), jnp.bfloat16),
            jax.ShapeDtypeStruct((STEPS * groups, channels, width), jnp.float32),
            jax.ShapeDtypeStruct((STEPS, nslab, width), jnp.float32),
        ],
        scratch_shapes=[columns, rotated, slab, pieces, pieces, slab, many, many, many, many, one, one],
        compiler_params=pltpu.CompilerParams(
            vmem_limit_bytes=56 << 20, collective_id=0, has_side_effects=True
        ),
    )(owners, sources, raw, kept, order, fine, slow)
    return pl.pallas_call(
        functools.partial(finish, coarse),
        grid=(STEPS, groups),
        in_specs=[
            pl.BlockSpec((GROUP - 1, channels, nslab, L), lambda s, g: (s * groups + g, 0, 0, 0)),
            pl.BlockSpec((1, channels, width), lambda s, g: (s * groups + g, 0, 0)),
            pl.BlockSpec((1, nslab, width), lambda s, g: (s, 0, 0)),
            pl.BlockSpec(fine.shape, lambda s, g: (0, 0, 0)),
            pl.BlockSpec(slow.shape, lambda s, g: (0, 0, 0)),
        ],
        out_specs=pl.BlockSpec((GROUP, channels, nslab, L), lambda s, g: (s * groups + g, 0, 0, 0)),
        out_shape=jax.ShapeDtypeStruct((STEPS * blocks, channels, nslab, L), jnp.bfloat16),
        scratch_shapes=[columns, rotated],
        compiler_params=pltpu.CompilerParams(vmem_limit_bytes=56 << 20),
    )(done, rows, slabs, fine, slow).reshape(STEPS, npanel, nslab, L)


def local(receiver_spectra, source_spectra, quality, slot_order, owners):
    bins = source_spectra.shape[2]
    raw = receiver_spectra.reshape(-1, 2 * bins)
    sources = source_spectra.reshape(-1, 2 * bins)
    kept = quality.astype(jnp.float32)[:, None]
    order = slot_order[0][:, None]
    my_owners = lax.dynamic_index_in_dim(owners, lax.axis_index("blk"), 1, keepdims=False)
    count, ring = lax.axis_size("cross"), lax.axis_size("blk")
    return correlate(my_owners, sources, raw, kept, order, count, ring)[:, None, None]


def solution(mesh):
    placed = (
        P(("blk", "cross"), None, None),
        P(("blk", "cross"), None, None),
        P(("blk", "cross")),
        P(("blk", "cross"), None),
        P(),
    )
    return jax.shard_map(
        local,
        mesh=mesh,
        in_specs=placed,
        out_specs=P(None, "blk", "cross", None, None, None),
        check_vma=False,
    )
```

```python
import functools
import math

import jax
import jax.numpy as jnp
import numpy as np
from jax import lax
from jax.experimental import pallas as pl
from jax.experimental.pallas import tpu as pltpu
from jax.sharding import PartitionSpec as P

L = 256
STEPS = 2
FINE = 16
PIECE = 8
HOP = 3
GROUP = 4
MESH = pl.DeviceIdType.MESH


def phase_tables(bins, coarse):
    bin_index = np.arange(bins, dtype=np.float64)[None, :]
    fine_angle = np.pi / bins * (np.arange(FINE)[:, None] + 0.5) * bin_index
    coarse_angle = np.pi / bins * (FINE * np.arange(coarse)[:, None]) * bin_index
    fine = np.stack([np.cos(fine_angle), np.sin(fine_angle)])
    slow = np.stack([np.cos(coarse_angle), np.sin(coarse_angle)]) / bins
    return jnp.asarray(fine, jnp.float32), jnp.asarray(slow, jnp.float32)


def ordered(spectra, kept, slot_order):
    mean_power = jnp.mean(spectra * spectra, axis=1, keepdims=True)
    scaled = spectra * lax.rsqrt(mean_power + 1e-06) * kept
    coarse_part = scaled.astype(jnp.bfloat16)
    fine_part = (scaled - coarse_part.astype(jnp.float32)).astype(jnp.bfloat16)
    count = spectra.shape[0]
    picks = slot_order == lax.broadcasted_iota(jnp.int32, (count, count), 1)
    picks = jnp.where(picks, 1.0, 0.0).astype(jnp.bfloat16)
    first = jnp.dot(picks, coarse_part, preferred_element_type=jnp.float32)
    return first + jnp.dot(picks, fine_part, preferred_element_type=jnp.float32)


def build_columns(slab, slow_ref, w_ref):
    bins = slow_ref.shape[2]
    slots = slab.shape[0]
    real, imag = slab[:, :bins], slab[:, bins:]
    for a in range(slow_ref.shape[1]):
        c, s = slow_ref[0, a : a + 1, :], slow_ref[1, a : a + 1, :]
        rc, rs, ic, is_ = real * c, real * s, imag * c, imag * s
        rows = slice(a * slots, (a + 1) * slots)
        w_ref[0, rows, :bins] = (rc + is_).astype(jnp.bfloat16)
        w_ref[0, rows, bins:] = (ic - rs).astype(jnp.bfloat16)
        w_ref[1, rows, :bins] = (rc - is_).astype(jnp.bfloat16)
        w_ref[1, rows, bins:] = (ic + rs).astype(jnp.bfloat16)


def build_rows(panel, fine_ref, x_ref):
    bins = fine_ref.shape[2]
    c, s = fine_ref[0], fine_ref[1]
    for p in range(panel.shape[0]):
        real, imag = panel[p : p + 1, :bins], panel[p : p + 1, bins:]
        rc, rs, ic, is_ = real * c, real * s, imag * c, imag * s
        rows = slice(p * FINE, (p + 1) * FINE)
        x_ref[0, rows, :bins] = (rc - is_).astype(jnp.bfloat16)
        x_ref[0, rows, bins:] = (rs + ic).astype(jnp.bfloat16)
        x_ref[1, rows, :bins] = (rc + is_).astype(jnp.bfloat16)
        x_ref[1, rows, bins:] = (ic - rs).astype(jnp.bfloat16)


def product(x_ref, w_ref, out_ref, sign, channels, slots, coarse):
    half = coarse * FINE
    found = lax.dot_general(
        x_ref[sign], w_ref[sign], (((1,), (1,)), ((), ())), preferred_element_type=jnp.float32
    )
    for p in range(channels):
        part = found[p * FINE : (p + 1) * FINE]
        lags = jnp.concatenate([part[:, a * slots : (a + 1) * slots] for a in range(coarse)], axis=0)
        out_ref[p, :, sign * half : (sign + 1) * half] = lags.T.astype(jnp.bfloat16)


def kernel(
    coarse, channels, count, ring, owner_ref, own_ref, raw_ref, kept_ref, order_ref, fine_ref, slow_ref,
    out_ref, rows_ref, slabs_ref, w_ref, x_ref, q_ref, low, high, near, low_send, low_recv, high_send, high_recv, q_send, q_recv,
):
    step, block = pl.program_id(0), pl.program_id(1)
    npanel, slots = own_ref.shape[0], q_ref.shape[0]
    per_step = npanel // PIECE
    total = STEPS * per_step
    per_block = channels // PIECE
    blocks = npanel // channels
    me, spot = lax.axis_index("cross"), lax.axis_index("blk")
    has_low, has_high = me > 0, me < count - 1
    following, previous = lax.rem(spot + 1, ring), lax.rem(spot + ring - 1, ring)

    def own_rows(j):
        return pl.ds(pl.multiple_of(lax.rem(j, per_step) * PIECE, PIECE), PIECE)

    def upward(j, source):
        return pltpu.make_async_remote_copy(
            src_ref=source, dst_ref=low.at[j], send_sem=low_send.at[j], recv_sem=low_recv.at[j],
            device_id={"blk": spot, "cross": me + 1}, device_id_type=MESH,
        )

    def downward(j, source):
        return pltpu.make_async_remote_copy(
            src_ref=source, dst_ref=high.at[j], send_sem=high_send.at[j], recv_sem=high_recv.at[j],
            device_id={"blk": spot, "cross": me - 1}, device_id_type=MESH,
        )

    def slab_copy():
        return pltpu.make_async_remote_copy(
            src_ref=q_ref, dst_ref=near, send_sem=q_send.at[0], recv_sem=q_recv.at[0],
            device_id={"blk": following, "cross": me}, device_id_type=MESH,
        )

    def relay(t):
        up, down = t - HOP * (me - 1), t - HOP * (count - 2 - me)
        up_on = has_low & (up >= 0) & (up < total)
        down_on = has_high & (down >= 0) & (down < total)

        @pl.when(up_on)
        def _():
            upward(up, low.at[up]).wait_recv()
            mine = owner_ref[up // per_step] == me
            low[up] = jnp.where(mine, own_ref[own_rows(up), :], low[up])

        @pl.when(down_on)
        def _():
            downward(down, high.at[down]).wait_recv()
            mine = owner_ref[down // per_step] == me
            high[down] = jnp.where(mine, own_ref[own_rows(down), :], high[down])

        @pl.when(up_on & has_high)
        def _():
            upward(up, low.at[up]).start()

        @pl.when(down_on & has_low)
        def _():
            downward(down, high.at[down]).start()

    lead = HOP * (count - 2) + per_block

    @pl.when((step == 0) & (block == 0))
    def _():
        barrier = pltpu.get_barrier_semaphore()
        pl.semaphore_signal(barrier, inc=1, device_id={"blk": following, "cross": me}, device_id_type=MESH)
        pl.semaphore_signal(barrier, inc=1, device_id={"blk": previous, "cross": me}, device_id_type=MESH)

        @pl.when(has_low)
        def _():
            pl.semaphore_signal(barrier, inc=1, device_id={"blk": spot, "cross": me - 1}, device_id_type=MESH)

        @pl.when(has_high)
        def _():
            pl.semaphore_signal(barrier, inc=1, device_id={"blk": spot, "cross": me + 1}, device_id_type=MESH)

        pl.semaphore_wait(barrier, 2 + has_low.astype(jnp.int32) + has_high.astype(jnp.int32))

        @pl.when(me == 0)
        def _():
            @pl.loop(0, total)
            def _(j):
                upward(j, own_ref.at[own_rows(j), :]).start()

        @pl.when(me == count - 1)
        def _():
            @pl.loop(0, total)
            def _(j):
                downward(j, own_ref.at[own_rows(j), :]).start()

        @pl.when(me == 0)
        def _():
            @pl.loop(0, total)
            def _(j):
                low[j] = own_ref[own_rows(j), :]

        @pl.when(me == count - 1)
        def _():
            @pl.loop(0, total)
            def _(j):
                high[j] = own_ref[own_rows(j), :]

        q_ref[...] = ordered(raw_ref[...], kept_ref[...], order_ref[...])
        slabs_ref[0] = q_ref[...]

        @pl.loop(0, per_block)
        def _(t):
            relay(t)

        build_columns(q_ref[...], slow_ref, w_ref)
        slab_copy().start()

        @pl.loop(per_block, lead)
        def _(t):
            relay(t)

    @pl.when((step == 1) & (block == 0))
    def _():
        slab_copy().wait()
        slabs_ref[1] = near[...]
        build_columns(near[...], slow_ref, w_ref)

    now = (step * blocks + block) * per_block
    above = owner_ref[step] > me
    panel = jnp.concatenate([jnp.where(above, high[now + j], low[now + j]) for j in range(per_block)], axis=0)
    mean_power = jnp.mean(panel * panel, axis=1, keepdims=True)
    panel = panel * lax.rsqrt(mean_power + 1e-06)
    later = lax.rem(block, GROUP) == GROUP - 1

    @pl.when(later)
    def _():
        rows_ref[0] = panel

    @pl.when(jnp.logical_not(later))
    def _():
        build_rows(panel, fine_ref, x_ref)

    for sign in range(2):
        @pl.when(jnp.logical_not(later))
        def _():
            product(x_ref, w_ref, out_ref.at[0], sign, channels, slots, coarse)

        for extra in range(per_block // 2):
            relay(now + lead + sign * (per_block // 2) + extra)

    @pl.when((step == STEPS - 1) & (block == blocks - 1))
    def _():
        @pl.when(has_high)
        def _():
            @pl.loop(0, total)
            def _(j):
                upward(j, low.at[j]).wait_send()

        @pl.when(has_low)
        def _():
            @pl.loop(0, total)
            def _(j):
                downward(j, high.at[j]).wait_send()


def finish(coarse, done_ref, rows_ref, slab_ref, fine_ref, slow_ref, out_ref, w_ref, x_ref):
    channels, slots = rows_ref.shape[1], slab_ref.shape[1]

    @pl.when(pl.program_id(1) == 0)
    def _():
        build_columns(slab_ref[0], slow_ref, w_ref)

    build_rows(rows_ref[0], fine_ref, x_ref)
    out_ref[: GROUP - 1] = done_ref[...]
    for sign in range(2):
        product(x_ref, w_ref, out_ref.at[GROUP - 1], sign, channels, slots, coarse)


def correlate(owners, sources, raw, kept, order, count, ring, channels=16):
    npanel, width = sources.shape
    nslab = raw.shape[0]
    coarse = L // 2 // FINE
    fine, slow = phase_tables(width // 2, coarse)
    total = STEPS * npanel // PIECE
    blocks = npanel // channels
    groups = blocks // GROUP
    whole = pl.BlockSpec(memory_space=pltpu.VMEM)
    pieces = pltpu.VMEM((total, PIECE, width), jnp.float32)
    slab = pltpu.VMEM((nslab, width), jnp.float32)
    many = pltpu.SemaphoreType.DMA((total,))
    one = pltpu.SemaphoreType.DMA((1,))
    columns = pltpu.VMEM((2, coarse * nslab, width), jnp.bfloat16)
    rotated = pltpu.VMEM((2, channels * FINE, width), jnp.bfloat16)
    kept_blocks = groups * (GROUP - 1)

    def kept_index(s, i):
        return (s * kept_blocks + i // GROUP * (GROUP - 1) + jnp.minimum(i % GROUP, GROUP - 2), 0, 0, 0)

    done, rows, slabs = pl.pallas_call(
        functools.partial(kernel, coarse, channels, count, ring),
        grid=(STEPS, blocks),
        in_specs=[pl.BlockSpec(memory_space=pltpu.SMEM)] + [whole] * 6,
        out_specs=[
            pl.BlockSpec((1, channels, nslab, L), kept_index),
            pl.BlockSpec((1, channels, width), lambda s, i: (s * groups + i // GROUP, 0, 0)),
            whole,
        ],
        out_shape=[
            jax.ShapeDtypeStruct((STEPS * kept_blocks, channels, nslab, L), jnp.bfloat16),
            jax.ShapeDtypeStruct((STEPS * groups, channels, width), jnp.float32),
            jax.ShapeDtypeStruct((STEPS, nslab, width), jnp.float32),
        ],
        scratch_shapes=[columns, rotated, slab, pieces, pieces, slab, many, many, many, many, one, one],
        compiler_params=pltpu.CompilerParams(
            vmem_limit_bytes=56 << 20, collective_id=0, has_side_effects=True
        ),
    )(owners, sources, raw, kept, order, fine, slow)
    return pl.pallas_call(
        functools.partial(finish, coarse),
        grid=(STEPS, groups),
        in_specs=[
            pl.BlockSpec((GROUP - 1, channels, nslab, L), lambda s, g: (s * groups + g, 0, 0, 0)),
            pl.BlockSpec((1, channels, width), lambda s, g: (s * groups + g, 0, 0)),
            pl.BlockSpec((1, nslab, width), lambda s, g: (s, 0, 0)),
            pl.BlockSpec(fine.shape, lambda s, g: (0, 0, 0)),
            pl.BlockSpec(slow.shape, lambda s, g: (0, 0, 0)),
        ],
        out_specs=pl.BlockSpec((GROUP, channels, nslab, L), lambda s, g: (s * groups + g, 0, 0, 0)),
        out_shape=jax.ShapeDtypeStruct((STEPS * blocks, channels, nslab, L), jnp.bfloat16),
        scratch_shapes=[columns, rotated],
        compiler_params=pltpu.CompilerParams(vmem_limit_bytes=56 << 20),
    )(done, rows, slabs, fine, slow).reshape(STEPS, npanel, nslab, L)


def local(receiver_spectra, source_spectra, quality, slot_order, owners):
    bins = source_spectra.shape[2]
    raw = receiver_spectra.reshape(-1, 2 * bins)
    sources = source_spectra.reshape(-1, 2 * bins)
    kept = quality.astype(jnp.float32)[:, None]
    order = slot_order[0][:, None]
    my_owners = lax.dynamic_index_in_dim(owners, lax.axis_index("blk"), 1, keepdims=False)
    count, ring = lax.axis_size("cross"), lax.axis_size("blk")
    return correlate(my_owners, sources, raw, kept, order, count, ring)[:, None, None]


def solution(mesh):
    placed = (
        P(("blk", "cross"), None, None),
        P(("blk", "cross"), None, None),
        P(("blk", "cross")),
        P(("blk", "cross"), None),
        P(),
    )
    return jax.shard_map(
        local,
        mesh=mesh,
        in_specs=placed,
        out_specs=P(None, "blk", "cross", None, None, None),
        check_vma=False,
    )
```
